32 devices in a mesh: dp: 4 (over y, core), expert: 2 (over x), mp: 4 (over z).
Axes of the slice: x: 2, y: 2, z: 4, core: 2. Of those that a mesh axis runs over, the one named last changes fastest.
Arguments:
- tokens: bfloat16 [6144, 768], P(('dp', 'expert')), may hold values from -6 to 6
- qkv_weight: bfloat16 [3, 768, 768], P(None, None, 'mp'), may hold values from -0.21875 to 0.21875
- proj_weight: bfloat16 [768, 768], P('mp'), may hold values from -0.625 to 0.625
- position_bias: float32 [32, 12], P(None, 'mp'), may hold values from -4 to 4
- attn_gain: float32 [768], replicated, may hold values from 0.5 to 1.5
- moe_gain: float32 [768], replicated, may hold values from 0.5 to 1.5
- router_weight: bfloat16 [768, 8], replicated, may hold values from -0.4375 to 0.4375
- expert_up: bfloat16 [8, 768, 3072], P('expert', None, 'mp'), may hold values from -0.21875 to 0.21875
- expert_down: bfloat16 [8, 3072, 768], P('expert', 'mp'), may hold values from -0.109375 to 0.109375
- lengths: int32 [4], P('dp'), may hold values from 384 to 1536, as said below
- routes: int32 [6144, 2], P(('dp', 'expert')), may hold values from 0 to 7, all different within a row; in each aligned block of 768 rows (0 to 767, 768 to 1535, ...) at most 384 rows name the same one
- buckets: int32 [1536], replicated, may hold values from 0 to 31, as said below
- cotangent: bfloat16 [6144, 768], P(('dp', 'expert')), may hold values from -6 to 6
Outputs:
- layer_out: bfloat16 [6144, 768], P(('dp', 'expert'))
- grad_tokens: bfloat16 [6144, 768], P(('dp', 'expert'))
- grad_qkv: float32 [3, 768, 768], P(None, None, 'mp')
- grad_proj: float32 [768, 768], P('mp')
- grad_bias: float32 [32, 12], P(None, 'mp')
- grad_attn: float32 [768], replicated
- grad_moe: float32 [768], replicated
- grad_router: float32 [768, 8], replicated
- grad_up: float32 [8, 768, 3072], P('expert', 'dp', 'mp')
- grad_down: float32 [8, 3072, 768], P('expert', 'mp', 'dp')
The draws below stay inside these ranges and needn't reach their ends.
Inputs may be any that keep to these rules, and one draw needn't show every extreme that they name: `routes`: in each aligned block of 768 rows, each expert is named by at most 384 rows, a bound that some block reaches; the two experts of a row differ. `lengths`: one sequence has exactly 1536 valid tokens and another exactly 384. buckets is non-decreasing in the distance, buckets[0] = 0, and every bucket is used.
All inputs are finite; a program needn't handle non-finite values.
Results may differ from the reference program's by a relative error of at most 0.02.
Values may be sent and summed in bfloat16 or wider, within the bound.
No kernel may reach another device: no remote copies, remote signals or barrier semaphores. Data moves between devices by JAX's collectives and lax.ppermute only.
A program may use at most 256 MiB of HBM per device.

```python
import math
import jax
import jax.numpy as jnp
import numpy as np
from jax import lax

D = 768
HEADS = 12
HD = 64
FF = 3072
NB = 32
TOK_DEV = 768
EXPERTS = 8
SEQS = 1
LEN = 1536
TOKENS = 6144
CAP = 384
N_DP = 4


def draw_lengths(key, part):
    total_seqs = N_DP * SEQS
    drawn = jax.random.randint(jax.random.fold_in(key, 11), (total_seqs,), LEN // 4, LEN + 1)
    first_pick = jax.random.randint(jax.random.fold_in(key, 12), (), 0, total_seqs)
    step_away = jax.random.randint(jax.random.fold_in(key, 13), (), 1, total_seqs)
    second_pick = (first_pick + step_away) % total_seqs
    places = jnp.arange(total_seqs)
    drawn = jnp.where(places == first_pick, LEN, drawn)
    drawn = jnp.where(places == second_pick, LEN // 4, drawn)
    return drawn.astype(jnp.int32)


def draw_buckets(key, part):
    marks = jax.random.permutation(jax.random.fold_in(key, 21), LEN - 1)[:NB - 1] + 1
    distance = jnp.arange(LEN)
    return jnp.sum((marks[None, :] <= distance[:, None]).astype(jnp.int32), axis=1).astype(jnp.int32)


def levels(own_key, dims, split, smallest, high):
    level, own = 1.0, jax.random.fold_in(own_key, 6)
    for axis_at, shards_of in split:
        draws = jnp.exp(jax.random.uniform(jax.random.fold_in(own, axis_at), (shards_of,), jnp.float32, smallest / len(split), high / len(split)))
        level = level * jnp.repeat(draws, dims[axis_at] // shards_of).reshape([-1 if axis == axis_at else 1 for axis in range(len(dims))])
    return level


def routed_block(own_key, own, number, rows, count, top, limit, slope):
    sequence = jax.random.permutation(own_key, count)
    crowded, common = portions_of(count, rows * top, limit, slope, True), portions_of(count, rows * top, limit, slope, False)
    places = jnp.arange(count)

    def named(tallies, offset_by):
        used = int((tallies > 0).sum())
        fixed = max(1, used // 4)
        moved = fixed + (places - fixed + offset_by * (used - fixed)) % max(1, count - fixed)
        return jnp.zeros((count,), jnp.int32).at[sequence[jnp.where(places < fixed, places, moved)]].set(jnp.asarray(tallies, jnp.int32))

    tallies = jnp.where(number % 4 == 0, named(crowded, number // 4), named(common, number - number // 4 - 1))
    mixed = jax.random.permutation(jax.random.fold_in(own, 3), count)
    donor, taker = mixed[0:count // 2 * 2:2], mixed[1:count // 2 * 2:2]
    margin = jnp.minimum(tallies[donor] - 1, limit - tallies[taker]) // 2
    margin = jnp.where((donor == sequence[0]) | (taker == sequence[0]) | (tallies[taker] == 0), 0, jnp.maximum(margin, 0))
    moved = jax.random.randint(jax.random.fold_in(own, 4), (count // 2,), 0, 1 << 20) % (margin + 1)
    tallies = tallies.at[donor].add(-moved).at[taker].add(moved)
    items = jnp.searchsorted(jnp.cumsum(tallies), jnp.arange(rows * top), side="right").astype(jnp.int32)
    listing = items.reshape(top, rows).T
    listing = listing[jax.random.permutation(jax.random.fold_in(own, 1), rows)]
    offset_by = jax.random.randint(jax.random.fold_in(own, 2), (rows, 1), 0, top)
    return jnp.take_along_axis(listing, (jnp.arange(top)[None, :] + offset_by) % top, axis=1)


def portions_of(number_of, total, limit, slope, full):
    portions = [(1 << 20) // math.isqrt(standing ** slope) + 1 for standing in range(1, number_of + 1)]
    largest = limit if full else min(limit, max(-(-total // number_of), total * portions[0] // sum(portions)))
    least = 1 if total - largest >= number_of - 1 else 0
    counts, surplus = [largest] + [least] * (number_of - 1), total - largest - least * (number_of - 1)
    while surplus > 0:
        free = [i for i in range(1, number_of) if counts[i] < largest] or [i for i in range(1, number_of) if counts[i] < limit]
        mass, budget = sum([portions[i] for i in free]), surplus
        for i in free:
            addition = min(limit - counts[i], max(1, budget * portions[i] // mass), surplus)
            counts[i] = counts[i] + addition
            surplus = surplus - addition
    return np.array(counts)


def centred(key, dims, deviation, bound, cuts=(), kind=jnp.bfloat16):
    values = jax.random.normal(key, dims, jnp.float32) * deviation
    if len(cuts) > 0:
        values = levels(key, dims, cuts, -0.22, 0.18) * values
    return jnp.clip(values, min=-bound, max=bound).astype(kind)


def setup_inputs(seed: int = 0) -> dict:
    key_list = jax.random.split(jax.random.key(seed), 14)
    tokens = centred(key_list[0], (TOKENS, D), 1.0, 6.0, ((0, 8),))
    qkv_weight = centred(key_list[1], (3, D, HEADS * HD), D ** -0.5, 0.21875, ((2, 4),))
    proj_weight = centred(key_list[2], (HEADS * HD, D), (HEADS * HD // 8) ** -0.5, 0.625, ((0, 4),))
    position_bias = centred(key_list[3], (NB, HEADS), 1.0, 4.0, ((1, 4),), jnp.float32)
    attn_gain = jnp.clip(1.0 + 0.1 * jax.random.normal(key_list[4], (D,), jnp.float32), 0.5, 1.5)
    moe_gain = jnp.clip(1.0 + 0.1 * jax.random.normal(key_list[5], (D,), jnp.float32), 0.5, 1.5)
    router_weight = centred(key_list[6], (D, EXPERTS), (D // 4) ** -0.5, 0.4375)
    expert_up = centred(key_list[7], (EXPERTS, D, FF), D ** -0.5, 0.21875, ((0, 2), (2, 4)))
    expert_down = centred(key_list[8], (EXPERTS, FF, D), FF ** -0.5, 0.109375, ((0, 2), (1, 4)))
    lengths = draw_lengths(jax.random.fold_in(key_list[13], 71), 0)
    routes_keys = jax.random.split(jax.random.fold_in(key_list[10], 1), TOKENS // TOK_DEV)
    routes_turns = jax.random.permutation(jax.random.fold_in(key_list[10], 3), TOKENS // TOK_DEV)
    routes = jax.vmap(lambda own, number: routed_block(jax.random.fold_in(key_list[10], 2), own, number, TOK_DEV, EXPERTS, 2, CAP, 1))(routes_keys, routes_turns).reshape((TOKENS, 2))
    buckets = draw_buckets(jax.random.fold_in(key_list[13], 71), 0)
    cotangent = centred(key_list[12], (TOKENS, D), 1.0, 6.0, ((0, 8),))
    return {"tokens": tokens, "qkv_weight": qkv_weight, "proj_weight": proj_weight, "position_bias": position_bias, "attn_gain": attn_gain, "moe_gain": moe_gain, "router_weight": router_weight, "expert_up": expert_up, "expert_down": expert_down, "lengths": lengths, "routes": routes, "buckets": buckets, "cotangent": cotangent}


@jax.custom_vjp
def low(v):
    return lax.optimization_barrier(v.astype(jnp.bfloat16)).astype(jnp.float32)

@jax.custom_vjp
def low_back(v):
    return v

def low_keep(v):
    return (low(v), None)

def low_pass(kept, grad):
    return (grad,)

def back_keep(v):
    return (v, None)

def back_low(kept, grad):
    return (low(grad),)
low.defvjp(low_keep, low_pass)
low_back.defvjp(back_keep, back_low)
EPS = 1e-06
NEG = -1e+30
HIGH = lax.Precision.HIGHEST

def norm_rows(values, gain):
    return values * lax.rsqrt(lax.optimization_barrier(jnp.mean(values * values, axis=-1, keepdims=True)) + EPS) * gain

def route_weights(logits, routes):
    router = jax.nn.softmax(logits, axis=-1)
    chosen = jnp.take_along_axis(router, routes, axis=1)
    return chosen / lax.optimization_barrier(jnp.sum(chosen, axis=1, keepdims=True))

def product(left, right):
    return jnp.dot(left, right, precision=HIGH)

def attend_block(query_block, block_start, keys_all, values_all, bias_table):
    raw_scores = low_back(jnp.einsum('hqd,hkd->hqk', query_block, keys_all, precision=HIGH))
    query_pos = block_start + jnp.arange(query_block.shape[1], dtype=jnp.int32)
    key_pos = jnp.arange(keys_all.shape[1], dtype=jnp.int32)
    distance = query_pos[:, None] - key_pos[None, :]
    offset = jnp.clip(distance, 0, keys_all.shape[1] - 1)
    scores = raw_scores * HD ** (-0.5) + jnp.take(bias_table, offset, axis=1)
    scores = jnp.where((distance >= 0)[None], scores, NEG)
    probs = jax.nn.softmax(scores, axis=-1)
    return low_back(low(jnp.einsum('hqk,hkd->hqd', low(probs), values_all, precision=HIGH)))

def attend_sequence(seq_input, qkv_weight, bias_table):
    queries = low_back(low(product(seq_input, qkv_weight[0])))
    keys_all = low_back(low(product(seq_input, qkv_weight[1])))
    values_all = low_back(low(product(seq_input, qkv_weight[2])))
    query_heads = queries.reshape(LEN, HEADS, HD).transpose(1, 0, 2)
    key_heads = keys_all.reshape(LEN, HEADS, HD).transpose(1, 0, 2)
    value_heads = values_all.reshape(LEN, HEADS, HD).transpose(1, 0, 2)
    block_rows = math.gcd(LEN, 512)
    block_count = LEN // block_rows
    query_blocks = query_heads.reshape(HEADS, block_count, block_rows, HD).transpose(1, 0, 2, 3)
    block_starts = jnp.arange(block_count, dtype=jnp.int32) * block_rows
    checked = jax.checkpoint(attend_block)
    outputs = lax.map(lambda pair_in: checked(pair_in[0], pair_in[1], key_heads, value_heads, bias_table), (query_blocks, block_starts))
    return outputs.transpose(0, 2, 1, 3).reshape(LEN, HEADS * HD)

def forward(token_values, qkv_weight, proj_weight, position_bias, attn_gain, moe_gain, router_weight, expert_up, expert_down, lengths, routes, buckets):
    attn_input = low(norm_rows(token_values, attn_gain))
    bias_table = jnp.take(position_bias, buckets, axis=0).T
    mixed = lax.map(lambda seq_input: attend_sequence(seq_input, qkv_weight, bias_table), attn_input.reshape(-1, LEN, D))
    attn_branch = low_back(product(mixed.reshape(-1, HEADS * HD), proj_weight))
    residual = token_values + attn_branch
    expert_input = low(norm_rows(residual, moe_gain))
    gate_weights = route_weights(product(expert_input, router_weight), routes)

    def one_expert(total, expert_index):
        coefficient = lax.optimization_barrier(jnp.sum(gate_weights * (routes == expert_index).astype(gate_weights.dtype), axis=1))
        pre_act = low_back(product(expert_input, expert_up[expert_index]))
        act_low = low(jax.nn.gelu(pre_act))
        expert_rows = low_back(product(act_low, expert_down[expert_index]))
        return (total + coefficient[:, None] * expert_rows, None)
    moe_branch, unused = lax.scan(jax.checkpoint(one_expert), jnp.zeros_like(token_values), jnp.arange(EXPERTS, dtype=jnp.int32))
    positions = jnp.arange(LEN, dtype=jnp.int32)
    valid = (positions[None, :] < lengths[:, None]).reshape(-1).astype(token_values.dtype)
    return valid[:, None] * (residual + moe_branch)

def reference(tokens, qkv_weight, proj_weight, position_bias, attn_gain, moe_gain, router_weight, expert_up, expert_down, lengths, routes, buckets, cotangent):
    primals = (tokens.astype(jnp.float32), qkv_weight.astype(jnp.float32), proj_weight.astype(jnp.float32), position_bias.astype(jnp.float32), attn_gain.astype(jnp.float32), moe_gain.astype(jnp.float32), router_weight.astype(jnp.float32), expert_up.astype(jnp.float32), expert_down.astype(jnp.float32))

    def closed(*values):
        return forward(*values, lengths, routes, buckets)
    layer_out, pullback = jax.vjp(closed, *primals)
    grads = pullback(cotangent.astype(jnp.float32))
    return (layer_out.astype(jnp.bfloat16), grads[0].astype(jnp.bfloat16), grads[1], grads[2], grads[3], grads[4], grads[5], grads[6], grads[7], grads[8])
```

```python
import functools
import math

import jax
import jax.numpy as jnp
from jax import lax
from jax.experimental import pallas as pl
from jax.experimental.pallas import tpu as pltpu
from jax.sharding import PartitionSpec as P

EPS = 1e-06
NEG = -1e30
HIGH = lax.Precision.HIGHEST


def norm_rows(values, gain):
    return values * lax.rsqrt(jnp.mean(values * values, axis=-1, keepdims=True) + EPS) * gain


def route_weights(logits, routes):
    router = jax.nn.softmax(logits, axis=-1)
    chosen = jnp.take_along_axis(router, routes, axis=1)
    return chosen / jnp.sum(chosen, axis=1, keepdims=True)


F32 = jnp.float32
BF16 = jnp.bfloat16
VMEM_LIMIT = 60 * 1024 * 1024
QT = 256
SUB = 128
ROWT = 128


def mm(a, b):
    return jnp.dot(a, b, preferred_element_type=F32)


def mm_t(a, b):
    return lax.dot_general(a, b, (((1,), (1,)), ((), ())), preferred_element_type=F32)


def t_mm(a, b):
    return lax.dot_general(a, b, (((0,), (0,)), ((), ())), preferred_element_type=F32)


def call(kernel, out_shape, in_specs, scratch=(), flops=0, nbytes=0, exps=0, **kw):
    return pl.pallas_call(
        kernel,
        out_shape=out_shape,
        in_specs=in_specs,
        scratch_shapes=scratch,
        compiler_params=pltpu.CompilerParams(vmem_limit_bytes=VMEM_LIMIT),
        cost_estimate=pl.CostEstimate(
            flops=int(flops), bytes_accessed=int(nbytes), transcendentals=int(exps)
        ),
        **kw,
    )


VM = pl.BlockSpec(memory_space=pltpu.VMEM)
SM = pl.BlockSpec(memory_space=pltpu.SMEM)


def sds(shape, dtype):
    return jax.ShapeDtypeStruct(shape, dtype)


def strip_kernel(start_ref, table_ref, out_ref):
    heads, rows, width = out_ref.shape
    seq = width - SUB
    spot = lax.broadcasted_iota(jnp.int32, (8, width), 1)
    dist = jnp.where(
        spot <= seq - SUB, seq - SUB - spot, jnp.where(spot > seq, 2 * seq - spot, 0)
    )
    for h in range(heads):
        value = jnp.full((8, width), table_ref[0, h], F32)
        for b in range(1, table_ref.shape[0]):
            value = jnp.where(dist >= start_ref[b], table_ref[b, h], value)
        wide = jnp.broadcast_to(value[0:1, :], (rows, width))
        out_ref[h] = pltpu.roll(wide, 0, 1, stride=1, stride_axis=0)


def head_lanes(h, width, head_size):
    lane = lax.broadcasted_iota(jnp.int32, (1, width), 1)
    return (lane >= h * head_size) & (lane < (h + 1) * head_size)


def bias_rows(strip_ref, h, off, length):
    parts = []
    for b in range(QT // SUB):
        start = off - b * SUB
        if not isinstance(start, int):
            start = pl.multiple_of(start, SUB)
        parts.append(strip_ref[h, :, pl.ds(start, length)])
    return jnp.concatenate(parts, axis=0)


def causal(scores, length):
    row = lax.broadcasted_iota(jnp.int32, (QT, QT), 0)
    col = lax.broadcasted_iota(jnp.int32, (QT, QT), 1)
    last = jnp.where(row >= col, scores[:, length - QT :], NEG)
    if length == QT:
        return last
    return jnp.concatenate([scores[:, : length - QT], last], axis=1)


def pick(stats, h):
    lane = lax.broadcasted_iota(jnp.int32, stats.shape, 1)
    return jnp.sum(jnp.where(lane == h, stats, 0.0), axis=1, keepdims=True)


def diag_fwd_kernel(head_size, heads, qkv_ref, strip_ref, acc_ref, m_ref, l_ref):
    rows, width = acc_ref.shape
    seq = strip_ref.shape[2] - SUB
    lane = lax.broadcasted_iota(jnp.int32, (QT, 128), 1)
    for i in range(rows // QT):
        length = (i + 1) * QT
        off = seq - SUB - i * QT
        here = slice(i * QT, (i + 1) * QT)

        def body(h, carry, length=length, off=off, here=here):
            acc, mx, ls = carry
            sel = head_lanes(h, width, head_size)
            q = qkv_ref[0, here, :] * jnp.where(sel, head_size**-0.5, 0.0).astype(BF16)
            v = qkv_ref[2, 0:length, :] * jnp.where(sel, 1.0, 0.0).astype(BF16)
            s = mm_t(q, qkv_ref[1, 0:length, :]) + bias_rows(strip_ref, h, off, length)
            s = causal(s, length)
            m = jnp.max(s, axis=1, keepdims=True)
            p = jnp.exp(s - m)
            l = jnp.sum(p, axis=1, keepdims=True)
            acc = acc + mm(p.astype(BF16), v)
            return (acc, jnp.where(lane == h, m, mx), jnp.where(lane == h, l, ls))

        zero = jnp.zeros((QT, 128), F32)
        acc, mx, ls = lax.fori_loop(
            0, heads, body, (jnp.zeros((QT, width), F32), zero, zero)
        )
        acc_ref[here, :] = acc
        m_ref[here, :] = mx
        l_ref[here, :] = ls


def cross_fwd_kernel(
    head_size, heads, at_ref, qkv_ref, kv_ref, strip_ref, acc_ref, m_ref, l_ref,
    o_ref, lse_ref, rel_ref, low_ref,
):
    rows, width = acc_ref.shape
    part = rel_ref.shape[1]
    lane = lax.broadcasted_iota(jnp.int32, (QT, 128), 1)

    @pl.when(at_ref[0] == 1)
    def _():
        def tile(i, unused):
            here = pl.ds(pl.multiple_of(i * QT, QT), QT)
            off = rows - SUB - i * QT
            acc_in = acc_ref[here, :]
            mx, ls = m_ref[here, :], l_ref[here, :]

            def body(h, carry):
                acc, lse = carry
                sel = head_lanes(h, width, head_size)
                q = qkv_ref[0, here, :] * jnp.where(sel, head_size**-0.5, 0.0).astype(BF16)
                v = kv_ref[1] * jnp.where(sel, 1.0, 0.0).astype(BF16)
                s = mm_t(q, kv_ref[0]) + bias_rows(strip_ref, h, off, rows)
                m_old, l_old = pick(mx, h), pick(ls, h)
                m = jnp.maximum(m_old, jnp.max(s, axis=1, keepdims=True))
                p = jnp.exp(s - m)
                alpha = jnp.exp(m_old - m)
                l = l_old * alpha + jnp.sum(p, axis=1, keepdims=True)
                inv = 1.0 / l
                new = mm(p.astype(BF16), v) * inv
                acc = acc + new + jnp.where(sel, acc_in * (alpha * inv), 0.0)
                return (acc, jnp.where(lane == h, m + jnp.log(l), lse))

            acc, lse = lax.fori_loop(
                0, heads, body, (jnp.zeros((QT, width), F32), jnp.zeros((QT, 128), F32))
            )
            o_ref[here, :] = acc
            lse_ref[here, :] = lse
            low_ref[here, :] = acc.astype(BF16)
            return unused

        lax.fori_loop(0, rows // QT, tile, 0)

    @pl.when(at_ref[0] == 0)
    def _():
        for i in range(rows // QT):
            here = slice(i * QT, (i + 1) * QT)
            acc = jnp.zeros((QT, width), F32)
            lse = jnp.zeros((QT, 128), F32)
            for h in range(heads):
                m, l = m_ref[here, h : h + 1], l_ref[here, h : h + 1]
                sel = head_lanes(h, width, head_size)
                acc = acc + jnp.where(sel, acc_ref[here, :] * (1.0 / l), 0.0)
                lse = jnp.where(lane == h, m + jnp.log(l), lse)
            o_ref[here, :] = acc
            lse_ref[here, :] = lse
            low_ref[here, :] = acc.astype(BF16)

    count = rel_ref.shape[0]
    for s in range(count):
        q = lax.rem(at_ref[1] + s, count)
        rel_ref[s] = low_ref[pl.ds(pl.multiple_of(q * part, part), part), :]


def grad_tile(head_size, h, here, length, off, qkv_ref, k_ref, v_ref, strip_ref, lse_ref,
              do_ref, o_ref, qt_ref, dot_ref, bacc_ref, dkt_ref, dvt_ref, diag):
    width = o_ref.shape[1]
    scale = head_size**-0.5
    sel = head_lanes(h, width, head_size)
    sel_scale = jnp.where(sel, scale, 0.0).astype(BF16)
    sel_one = jnp.where(sel, 1.0, 0.0).astype(BF16)
    q = qkv_ref[0, here, :] * sel_scale
    d_o = do_ref[here, :] * sel_one
    k, v = k_ref[0:length, :], v_ref[0:length, :]
    s = mm_t(q, k) + bias_rows(strip_ref, h, off, length)
    if diag:
        s = causal(s, length)
    p = jnp.exp(s - pick(lse_ref[here, :], h))
    delta = jnp.sum(d_o.astype(F32) * o_ref[here, :], axis=1, keepdims=True)
    ds = p * (mm_t(d_o, v) - delta)
    for b in range(QT // SUB):
        start = off - b * SUB
        if not isinstance(start, int):
            start = pl.multiple_of(start, SUB)
        at = pl.ds(start, length)
        bacc_ref[h, :, at] = bacc_ref[h, :, at] + ds[b * SUB : (b + 1) * SUB, :]
    ds_low, p_low = ds.astype(BF16), p.astype(BF16)
    hrows = pl.ds(pl.multiple_of(h * head_size, head_size), head_size)
    dkt_ref[hrows, 0:length] = dkt_ref[hrows, 0:length] + mm(qt_ref[hrows, here], ds_low)
    dvt_ref[hrows, 0:length] = dvt_ref[hrows, 0:length] + mm(dot_ref[hrows, here], p_low)
    return mm(ds_low, k * sel_scale)


def ordered(at_ref, pieces, out_ref):
    count, part = len(pieces), pieces[0].shape[0]
    for s, piece in enumerate(pieces):
        q = lax.rem(at_ref[1] + s, count)
        out_ref[pl.ds(pl.multiple_of(q * part, part), part), :] = piece[...]


def to_relative(at_ref, value_t, scr_ref, out_ref, count):
    scr_ref[...] = value_t
    part = scr_ref.shape[0] // count
    for s in range(count):
        q = lax.rem(at_ref[1] + count - s, count)
        out_ref[s * part : (s + 1) * part, :] = scr_ref[
            pl.ds(pl.multiple_of(q * part, part), part), :
        ].astype(out_ref.dtype)


def cross_bwd_kernel(
    head_size, heads, at_ref, qkv_ref, kv_ref, strip_ref, lse_ref, o_ref, p0, p1, p2, p3,
    dq_ref, dkv_ref, bacc_ref, do_ref, qt_ref, dot_ref, dkt_ref, dvt_ref, scr_ref,
):
    rows, width = o_ref.shape
    ordered(at_ref, (p0, p1, p2, p3), do_ref)
    bacc_ref[...] = jnp.zeros_like(bacc_ref)

    @pl.when(at_ref[0] == 1)
    def _():
        qt_ref[...] = (qkv_ref[0].astype(F32) * head_size**-0.5).T.astype(BF16)
        dot_ref[...] = do_ref[...].astype(F32).T.astype(BF16)
        dkt_ref[...] = jnp.zeros_like(dkt_ref)
        dvt_ref[...] = jnp.zeros_like(dvt_ref)
        for i in range(rows // QT):
            here = slice(i * QT, (i + 1) * QT)
            off = rows - SUB - i * QT

            def body(h, dq, here=here, off=off):
                return dq + grad_tile(
                    head_size, h, here, rows, off, qkv_ref, kv_ref.at[0], kv_ref.at[1],
                    strip_ref, lse_ref, do_ref, o_ref, qt_ref, dot_ref, bacc_ref, dkt_ref,
                    dvt_ref, False,
                )

            dq_ref[here, :] = lax.fori_loop(0, heads, body, jnp.zeros((QT, width), F32))
        to_relative(at_ref, dkt_ref[...].T, scr_ref, dkv_ref.at[0], 4)
        to_relative(at_ref, dvt_ref[...].T, scr_ref, dkv_ref.at[1], 4)

    @pl.when(at_ref[0] == 0)
    def _():
        dq_ref[...] = jnp.zeros_like(dq_ref)
        dkv_ref[...] = jnp.zeros_like(dkv_ref)


def diag_bwd_kernel(
    head_size, heads, at_ref, qkv_ref, strip_ref, lse_ref, o_ref, do_ref, dqc_ref, baccin_ref,
    dqr_ref, dkv_ref, dist_ref, bacc_ref, dq_ref, qt_ref, dot_ref, dkt_ref, dvt_ref, scr_ref,
):
    rows, width = o_ref.shape
    seq = strip_ref.shape[2] - SUB
    bacc_ref[...] = baccin_ref[...]
    qt_ref[...] = (qkv_ref[0].astype(F32) * head_size**-0.5).T.astype(BF16)
    dot_ref[...] = do_ref[...].astype(F32).T.astype(BF16)
    dkt_ref[...] = jnp.zeros_like(dkt_ref)
    dvt_ref[...] = jnp.zeros_like(dvt_ref)
    for i in range(rows // QT):
        here = slice(i * QT, (i + 1) * QT)
        length = (i + 1) * QT
        off = seq - SUB - i * QT

        def body(h, dq, here=here, off=off, length=length):
            return dq + grad_tile(
                head_size, h, here, length, off, qkv_ref, qkv_ref.at[1], qkv_ref.at[2],
                strip_ref, lse_ref, do_ref, o_ref, qt_ref, dot_ref, bacc_ref, dkt_ref,
                dvt_ref, True,
            )

        dq_ref[here, :] = lax.fori_loop(0, heads, body, dqc_ref[here, :])
    to_relative(at_ref, dq_ref[...], scr_ref, dqr_ref, 4)
    to_relative(at_ref, dkt_ref[...].T, scr_ref, dkv_ref.at[0], 4)
    to_relative(at_ref, dvt_ref[...].T, scr_ref, dkv_ref.at[1], 4)
    span = bacc_ref.shape[2]
    row = lax.broadcasted_iota(jnp.int32, (SUB, span), 0)
    dist_ref[...] = jnp.zeros_like(dist_ref)
    for h in range(heads):
        acc = bacc_ref[h]
        for b in range(7):
            acc = jnp.where((row >> b) & 1 == 1, pltpu.roll(acc, span - (1 << b), 1), acc)
        dist_ref[h : h + 1, :] = jnp.sum(acc, axis=0, keepdims=True)


def residual_kernel(m0, m1, m2, m3, w0, w1, w2, w3, tok_ref, gain_ref, res_ref, in_ref):
    acc = tok_ref[...].astype(F32)
    for m, w in ((m0, w0), (m1, w1), (m2, w2), (m3, w3)):
        acc = acc + mm(m[...], w[...])
    res_ref[...] = acc
    r = lax.rsqrt(jnp.mean(acc * acc, axis=1, keepdims=True) + EPS)
    in_ref[...] = (acc * r * gain_ref[...]).astype(BF16)


def norm_grad(value, gain, grad):
    r = lax.rsqrt(jnp.mean(value * value, axis=1, keepdims=True) + EPS)
    scaled = grad * gain
    back = r * scaled - value * (r * r * r * jnp.mean(value * scaled, axis=1, keepdims=True))
    return back, jnp.sum(grad * value * r, axis=0, keepdims=True)


def residual_grad_kernel(
    b0, b1, b2, b3, res_ref, gain_ref, g_ref, m0, m1, m2, m3, w0, w1, w2, w3,
    dres_ref, d0, d1, d2, d3, gproj_ref, gmoe_ref,
):
    d_b = b0[...].astype(F32) + b1[...].astype(F32) + b2[...].astype(F32) + b3[...].astype(F32)
    back, gmoe = norm_grad(res_ref[...], gain_ref[...], d_b)
    d_res = g_ref[...].astype(F32) + back
    dres_ref[...] = d_res
    gmoe_ref[...] = jnp.broadcast_to(gmoe, gmoe_ref.shape)
    low = d_res.astype(BF16)
    for d, w in ((d0, w0), (d1, w1), (d2, w2), (d3, w3)):
        d[...] = mm_t(low, w[...]).astype(BF16)
    for s, m in enumerate((m0, m1, m2, m3)):
        gproj_ref[s] = t_mm(m[...], low).astype(BF16)


def token_grad_kernel(a0, a1, a2, a3, tok_ref, gain_ref, dres_ref, out_ref, gattn_ref):
    d_a = a0[...].astype(F32) + a1[...].astype(F32) + a2[...].astype(F32) + a3[...].astype(F32)
    back, gattn = norm_grad(tok_ref[...].astype(F32), gain_ref[...], d_a)
    out_ref[...] = (dres_ref[...] + back).astype(BF16)
    gattn_ref[...] = jnp.broadcast_to(gattn, gattn_ref.shape)


def output_kernel(at_ref, c0, c1, c2, c3, res_ref, out_ref):
    total = res_ref[...]
    for c in (c0, c1, c2, c3):
        total = total + c[...].astype(F32)
    rows = total.shape[0]
    pos = at_ref[3] + lax.broadcasted_iota(jnp.int32, (rows, 1), 0)
    out_ref[...] = jnp.where(pos < at_ref[4], total, 0.0).astype(BF16)


def gather_kernel(at_ref, p0, p1, p2, p3, out_ref):
    for s, p in enumerate((p0, p1, p2, p3)):
        out_ref[lax.rem(at_ref[1] + 4 - s, 4)] = p[...]


def one_hot_rows(rank_row, start, rows):
    spot = start + lax.broadcasted_iota(jnp.int32, (rows, rank_row.shape[1]), 0)
    return jnp.where(spot == rank_row, 1.0, 0.0).astype(BF16)


def scatter_matrix(rank_ref, s, out_ref, cap):
    tokens = rank_ref.shape[1]
    spot = lax.broadcasted_iota(jnp.int32, (tokens, cap), 1)
    for j in range(out_ref.shape[1] // cap):
        hit = spot == rank_ref[s, :, j : j + 1]
        out_ref[:, j * cap : (j + 1) * cap] = jnp.where(hit, 1.0, 0.0).astype(BF16)


def moe_pre_kernel(counts_ref, rank_ref, gown_ref, goth_ref, down_ref, g_out, d_out):
    j = pl.program_id(0)
    g_out[...] = jnp.zeros_like(g_out)
    d_out[...] = jnp.zeros_like(d_out)
    for s, src in enumerate((gown_ref, goth_ref)):
        rank_row = rank_ref[s, pl.ds(j, 1), :]

        def tile(i, unused, s=s, src=src, rank_row=rank_row):
            at = pl.ds(pl.multiple_of(i * ROWT, ROWT), ROWT)
            packed = mm(one_hot_rows(rank_row, i * ROWT, ROWT), src[...]).astype(BF16)
            g_out[s, 0, at, :] = packed
            d_out[s, 0, at, :] = mm_t(packed, down_ref[0]).astype(BF16)
            return unused

        lax.fori_loop(0, (counts_ref[s, j] + ROWT - 1) // ROWT, tile, 0)


GELU_C = math.sqrt(2.0 / math.pi)
GELU_A = 0.044715


def moe_main_kernel(
    at_ref, counts_ref, rank_ref, rankc_ref, routes_ref, router_ref, routert_ref,
    e0, e1, e2, e3, f0, f1, f2, f3, up_ref, d_ref,
    x_out, act_out, dpre_out, gate_out, own_out, oth_out, dl_out,
    e_scr, gate_scr, split_scr, dots_scr, dx_scr, scat_scr,
):
    j = pl.program_id(0)
    tokens, part = e_scr.shape[1], e0.shape[0]
    cap = x_out.shape[2]
    experts_here = pl.num_programs(0)
    lane = lax.broadcasted_iota(jnp.int32, (tokens, 128), 1)
    total = at_ref[5]

    @pl.when(j == 0)
    def _():
        for s, pieces in enumerate(((e0, e1, e2, e3), (f0, f1, f2, f3))):
            for b, piece in enumerate(pieces):
                e_scr[s, b * part : (b + 1) * part, :] = piece[...]
        dx_scr[...] = jnp.zeros_like(dx_scr)
        dots_scr[...] = jnp.zeros_like(dots_scr)
        for s in range(2):
            logits = mm(e_scr[s], router_ref[...])
            hit = (lane == routes_ref[s, :, 0:1]) | (lane == routes_ref[s, :, 1:2])
            top = jnp.max(jnp.where(hit, logits, NEG), axis=1, keepdims=True)
            ex = jnp.where(hit, jnp.exp(logits - top), 0.0)
            gate = ex / jnp.sum(ex, axis=1, keepdims=True)
            gate_scr[s] = gate
            high = gate.astype(BF16).astype(F32)
            low = gate - high
            split_scr[s] = (high + pltpu.roll(low, 64, 1)).astype(BF16)

    x_out[...] = jnp.zeros_like(x_out)
    act_out[...] = jnp.zeros_like(act_out)
    dpre_out[...] = jnp.zeros_like(dpre_out)
    gate_out[...] = jnp.zeros_like(gate_out)
    expert = total + j
    for s in range(2):
        rank_row = rank_ref[s, pl.ds(j, 1), :]

        def tile(i, unused, s=s, rank_row=rank_row):
            at = pl.ds(pl.multiple_of(i * ROWT, ROWT), ROWT)
            hot = one_hot_rows(rank_row, i * ROWT, ROWT)
            xs = mm(hot, e_scr[s]).astype(BF16)
            x_out[s, 0, at, :] = xs
            lane_t = lax.broadcasted_iota(jnp.int32, (ROWT, 128), 1)
            mine = (lane_t == expert) | (lane_t == expert + 64)
            gate = jnp.sum(
                jnp.where(mine, mm(hot, split_scr[s]), 0.0), axis=1, keepdims=True
            )
            gate_out[s, 0, at, :] = jnp.broadcast_to(gate, (ROWT, 128))
            pre = mm(xs, up_ref[0])
            sq = pre * pre
            th = jnp.tanh(GELU_C * pre * (1.0 + GELU_A * sq))
            half = 0.5 * (1.0 + th)
            act = (pre * half).astype(BF16)
            slope = half + (0.5 * GELU_C) * pre * (1.0 - th * th) * (1.0 + 3.0 * GELU_A * sq)
            act_out[s, 0, at, :] = act
            d_act = d_ref[s, 0, at, :].astype(F32)
            dots = jnp.sum(act.astype(F32) * d_act, axis=1, keepdims=True)
            dpre = (gate * d_act * slope).astype(BF16)
            dpre_out[s, 0, at, :] = dpre
            dx_at = pl.ds(pl.multiple_of(j * cap + i * ROWT, ROWT), ROWT)
            dx_scr[s, dx_at, :] = mm_t(dpre, up_ref[0]).astype(BF16)
            high = dots.astype(BF16).astype(F32)
            low = dots - high
            cols = jnp.where(lane_t == expert, high, jnp.where(lane_t == expert + 64, low, 0.0))
            dots_scr[s, dx_at, :] = cols.astype(BF16)
            return unused

        lax.fori_loop(0, (counts_ref[s, j] + ROWT - 1) // ROWT, tile, 0)

    @pl.when(j == experts_here - 1)
    def _():
        for s, out in enumerate((own_out, oth_out)):
            scatter_matrix(rankc_ref, s, scat_scr, cap)
            both = mm(scat_scr[...], dots_scr[s])
            dots = both + pltpu.roll(both, 64, 1)
            gate = gate_scr[s]
            mean = jnp.sum(gate * dots, axis=1, keepdims=True)
            d_logit = gate * (dots - mean)
            high = d_logit.astype(BF16).astype(F32)
            low = d_logit - high
            split = (high + pltpu.roll(low, 64, 1)).astype(BF16)
            dl_out[s] = split
            d_b = mm(scat_scr[...], dx_scr[s]) + mm(split, routert_ref[...])
            out[...] = d_b.astype(BF16)


def moe_post_kernel(
    at_ref, counts_ref, rankc_ref, x_ref, act_ref, dpre_ref, g_ref, gate_ref, down_ref,
    grad_out, own_out, oth_out, y_scr, scat_scr,
):
    j = pl.program_id(0)
    cap = x_ref.shape[2]
    model = x_ref.shape[3]
    part = model // 4

    @pl.when(j == 0)
    def _():
        y_scr[...] = jnp.zeros_like(y_scr)

    up = None
    down = None
    for s in range(2):

        def tile(i, unused, s=s):
            at = pl.ds(pl.multiple_of(i * ROWT, ROWT), ROWT)
            gate = gate_ref[s, 0, at, 0:1]
            y_at = pl.ds(pl.multiple_of(j * cap + i * ROWT, ROWT), ROWT)
            y_scr[s, y_at, :] = (gate * mm(act_ref[s, 0, at, :], down_ref[0])).astype(BF16)
            return unused

        lax.fori_loop(0, (counts_ref[s, j] + ROWT - 1) // ROWT, tile, 0)
        d_out = (gate_ref[s, 0, :, 0:1] * g_ref[s, 0].astype(F32)).astype(BF16)
        up_s = t_mm(x_ref[s, 0], dpre_ref[s, 0])
        down_s = t_mm(d_out, act_ref[s, 0])
        up = up_s if up is None else up + up_s
        down = down_s if down is None else down + down_s
    for q in range(4):
        rho = at_ref[2] ^ q
        slot = (rho & 1) * 2 + (rho >> 1)
        grad_out[slot, 0, 0] = up[q * part : (q + 1) * part, :].astype(BF16)
        grad_out[slot, 1, 0] = down[q * part : (q + 1) * part, :].astype(BF16)

    @pl.when(j == pl.num_programs(0) - 1)
    def _():
        for s, out in enumerate((own_out, oth_out)):
            scatter_matrix(rankc_ref, s, scat_scr, cap)
            out[...] = mm(scat_scr[...], y_scr[s]).astype(BF16)


def rot(shift):
    return [(i, (i + shift) % 4) for i in range(4)]


SWAP = [(0, 1), (1, 0)]
CORE = [(0, 1), (1, 0), (2, 3), (3, 2)]
YAX = [(0, 2), (2, 0), (1, 3), (3, 1)]


def add_low(a, b):
    return (a.astype(F32) + b.astype(F32)).astype(BF16)


def reduce_all(value, axis):
    half = value.shape[axis] // 2
    core = lax.axis_index("dp") % 2
    keep = lax.dynamic_slice_in_dim(value, core * half, half, axis)
    give = lax.dynamic_slice_in_dim(value, (1 - core) * half, half, axis)
    total = add_low(keep, lax.ppermute(give, "dp", CORE))
    total = add_low(total, lax.ppermute(total, "dp", YAX))
    return add_low(total, lax.ppermute(total, "expert", SWAP))


def join_cores(total, axis):
    other = lax.ppermute(total, "dp", CORE)
    first = lax.axis_index("dp") % 2 == 0
    low = jnp.where(first, total, other)
    high = jnp.where(first, other, total)
    return jnp.concatenate([low, high], axis=axis)


def fast_device(
    tokens, qkv_weight, proj_weight, position_bias, attn_gain, moe_gain, router_weight,
    expert_up, expert_down, lengths, routes, buckets, cotangent,
):
    rows, model = tokens.shape
    heads = position_bias.shape[1]
    table = position_bias.shape[0]
    width = proj_weight.shape[0]
    head_size = width // heads
    seq = buckets.shape[0]
    part = rows // 4
    x = lax.axis_index("expert")
    z = lax.axis_index("mp")
    dp = lax.axis_index("dp")
    experts = router_weight.shape[1]
    here = expert_up.shape[0]
    hidden = expert_up.shape[2]
    cap = 4 * rows // experts
    span = seq + SUB

    at = jnp.stack([
        x, z, dp, x * rows + z * part, lengths[0], x * here
    ]).astype(jnp.int32)

    token_values = tokens.astype(F32)
    attn_input = norm_rows(token_values, attn_gain).astype(BF16)
    qkv = jnp.einsum("td,cdf->ctf", attn_input, qkv_weight, preferred_element_type=F32).astype(BF16)
    kv_peer = lax.ppermute(qkv[1:3], "expert", [(0, 1)])

    starts = jnp.sum(
        (buckets[None, :] < jnp.arange(table, dtype=jnp.int32)[:, None]).astype(jnp.int32), axis=1
    )
    strip = call(
        strip_kernel, sds((heads, SUB, span), F32), [SM, SM], flops=1e6, nbytes=heads * SUB * span * 4
    )(starts, position_bias)
    acc, mx, ls = call(
        functools.partial(diag_fwd_kernel, head_size, heads),
        (sds((rows, width), F32), sds((rows, 128), F32), sds((rows, 128), F32)),
        [VM, VM],
        flops=4e9, nbytes=6e6, exps=rows * rows * heads,
    )(qkv, strip)
    mixed32, lse, mixed_rel = call(
        functools.partial(cross_fwd_kernel, head_size, heads),
        (sds((rows, width), F32), sds((rows, 128), F32), sds((4, part, width), BF16)),
        [SM] + [VM] * 6,
        [pltpu.VMEM((rows, width), BF16)],
        flops=4e9, nbytes=6e6, exps=rows * rows * heads,
    )(at, qkv, kv_peer, strip, acc, mx, ls)

    row_at = x * rows + jnp.arange(rows, dtype=jnp.int32)
    g_low = jnp.where((row_at < lengths[0])[:, None], cotangent, jnp.zeros_like(cotangent))
    order = (z + 4 - jnp.arange(4)) % 4

    def relative(value):
        blocks = value.reshape((4, part) + value.shape[1:])
        return jnp.concatenate(
            [lax.dynamic_index_in_dim(blocks, order[s], 0, False) for s in range(4)], axis=0
        )

    g_own, routes_own = relative(g_low), relative(routes)
    g_own_send, kv_peer_dep = lax.optimization_barrier((g_own, kv_peer))
    g_oth = lax.ppermute(g_own_send, "expert", SWAP)
    routes_oth = lax.ppermute(routes_own, "expert", SWAP)
    routes_both = jnp.stack([routes_own, routes_oth])
    mine = x * here + jnp.arange(here, dtype=jnp.int32)
    hits = jnp.any(routes_both[:, :, :, None] == mine, axis=2)
    hits_t = hits.transpose(0, 2, 1).reshape(2 * here, rows).astype(BF16)
    before = (jnp.arange(rows)[:, None] < jnp.arange(rows)[None, :]).astype(BF16)
    ranks = jnp.dot(hits_t, before, preferred_element_type=F32)
    rank_row = jnp.where(hits_t > 0, ranks, -1.0).astype(jnp.int32).reshape(2, here, rows)
    rank_col = rank_row.transpose(0, 2, 1)
    counts = jnp.sum(hits.astype(jnp.int32), axis=1)

    whole = lambda shape: pl.BlockSpec(shape, lambda j, n=len(shape): (0,) * n)
    packed_spec = lambda last: pl.BlockSpec((2, 1, cap, last), lambda j: (0, j, 0, 0))
    weight_spec = lambda a, b: pl.BlockSpec((1, a, b), lambda j: (j, 0, 0))
    unit = 2.0 * 2 * rows * 2 * hidden * model / 2
    g_pack, d_pack = call(
        moe_pre_kernel,
        (sds((2, here, cap, model), BF16), sds((2, here, cap, hidden), BF16)),
        [SM, whole((2, here, rows)), whole((rows, model)), whole((rows, model)),
         weight_spec(hidden, model)],
        flops=2 * unit, nbytes=16e6,
        grid=(here,),
        out_specs=(packed_spec(model), packed_spec(hidden)),
    )(counts, rank_row, g_own, g_oth, expert_down)

    proj = [proj_weight] + [lax.ppermute(proj_weight, "mp", rot(s)) for s in (1, 2, 3)]
    mixed = [mixed_rel[0]] + [lax.ppermute(mixed_rel[s], "mp", rot(s)) for s in (1, 2, 3)]
    tok_part = lax.dynamic_slice_in_dim(tokens, z * part, part, 0)
    residual, e_part = call(
        residual_kernel,
        (sds((part, model), F32), sds((part, model), BF16)),
        [VM] * 10,
        flops=2 * part * model * model, nbytes=4e6,
    )(*mixed, *proj, tok_part, moe_gain[None, :])

    e_own = [e_part] + [lax.ppermute(e_part, "mp", rot(s)) for s in (1, 2, 3)]
    e_oth = [lax.ppermute(piece, "expert", SWAP) for piece in e_own]

    pad = jnp.zeros((model, 64 - experts), BF16)
    router_cols = jnp.concatenate([router_weight, pad, jnp.zeros((model, 64), BF16)], axis=1)
    router_rows = jnp.concatenate([router_weight, pad, router_weight, pad], axis=1).T
    x_pack, act_pack, dpre_pack, gate_pack, db_own, db_oth, dl = call(
        moe_main_kernel,
        (
            sds((2, here, cap, model), BF16),
            sds((2, here, cap, hidden), BF16),
            sds((2, here, cap, hidden), BF16),
            sds((2, here, cap, 128), F32),
            sds((rows, model), BF16),
            sds((rows, model), BF16),
            sds((2, rows, 128), BF16),
        ),
        [SM, SM, whole((2, here, rows)), whole((2, rows, here)), whole((2, rows, 2)),
         whole((model, 128)), whole((128, model))]
        + [whole((part, model))] * 8
        + [weight_spec(model, hidden), packed_spec(hidden)],
        [
            pltpu.VMEM((2, rows, model), BF16),
            pltpu.VMEM((2, rows, 128), F32),
            pltpu.VMEM((2, rows, 128), BF16),
            pltpu.VMEM((2, here * cap, 128), BF16),
            pltpu.VMEM((2, here * cap, model), BF16),
            pltpu.VMEM((rows, here * cap), BF16),
        ],
        flops=4 * unit, nbytes=24e6,
        grid=(here,),
        out_specs=(
            packed_spec(model), packed_spec(hidden), packed_spec(hidden), packed_spec(128),
            whole((rows, model)), whole((rows, model)), whole((2, rows, 128)),
        ),
    )(at, counts, rank_row, rank_col, routes_both, router_cols, router_rows,
      *e_own, *e_oth, expert_up, d_pack)

    db_sum = add_low(db_own, lax.ppermute(db_oth, "expert", SWAP)).reshape(4, part, model)
    db = [db_sum[0]] + [lax.ppermute(db_sum[s], "mp", rot(-s)) for s in (1, 2, 3)]

    grads, out_own, out_oth = call(
        moe_post_kernel,
        (
            sds((4, 2, here, model // 4, hidden), BF16),
            sds((rows, model), BF16),
            sds((rows, model), BF16),
        ),
        [SM, SM, whole((2, rows, here)), packed_spec(model), packed_spec(hidden),
         packed_spec(hidden), packed_spec(model), packed_spec(128), weight_spec(hidden, model)],
        [pltpu.VMEM((2, here * cap, model), BF16), pltpu.VMEM((rows, here * cap), BF16)],
        flops=4 * unit, nbytes=30e6,
        grid=(here,),
        out_specs=(
            pl.BlockSpec((4, 2, 1, model // 4, hidden), lambda j: (0, 0, j, 0, 0)),
            whole((rows, model)), whole((rows, model)),
        ),
    )(at, counts, rank_col, x_pack, act_pack, dpre_pack, g_pack, gate_pack, expert_down)

    d_res, dm0, dm1, dm2, dm3, gproj, gmoe = call(
        residual_grad_kernel,
        (sds((part, model), F32),) + (sds((part, width), BF16),) * 4
        + (sds((4, width, model), BF16), sds((8, model), F32)),
        [VM] * 15,
        flops=4 * part * model * model, nbytes=5e6,
    )(*db, residual, moe_gain[None, :], g_own[:part], *mixed, *proj)
    d_mixed = [dm0] + [
        lax.ppermute(piece, "mp", rot(-s)) for s, piece in ((1, dm1), (2, dm2), (3, dm3))
    ]

    scratch = [
        pltpu.VMEM((width, rows), BF16), pltpu.VMEM((width, rows), BF16),
        pltpu.VMEM((width, rows), F32), pltpu.VMEM((width, rows), F32),
        pltpu.VMEM((rows, width), F32),
    ]
    dq_cross, dkv_peer, bias_acc, d_o = call(
        functools.partial(cross_bwd_kernel, head_size, heads),
        (sds((rows, width), F32), sds((2, rows, width), BF16), sds((heads, SUB, span), F32),
         sds((rows, width), BF16)),
        [SM] + [VM] * 9,
        scratch,
        flops=8e9, nbytes=10e6, exps=rows * rows * heads,
    )(at, qkv, kv_peer, strip, lse, mixed32, *d_mixed)
    dkv_back = lax.ppermute(dkv_peer, "expert", [(1, 0)])
    dq, dkv, dist = call(
        functools.partial(diag_bwd_kernel, head_size, heads),
        (sds((rows, width), BF16), sds((2, rows, width), F32), sds((8, span), F32)),
        [SM] + [VM] * 7,
        [pltpu.VMEM((heads, SUB, span), F32), pltpu.VMEM((rows, width), F32)] + scratch,
        flops=8e9, nbytes=10e6, exps=rows * rows * heads,
    )(at, qkv, strip, lse, mixed32, d_o, dq_cross, bias_acc)
    dkv_low = add_low(dkv, dkv_back)
    dqkv = jnp.concatenate([dq[None], dkv_low], axis=0)
    da = jnp.einsum(
        "ctf,cdf->td", dqkv, qkv_weight, preferred_element_type=F32
    ).astype(BF16).reshape(4, part, model)
    da_parts = [da[0]] + [lax.ppermute(da[s], "mp", rot(-s)) for s in (1, 2, 3)]
    gtok, gattn = call(
        token_grad_kernel,
        (sds((part, model), BF16), sds((8, model), F32)),
        [VM] * 7,
        nbytes=3e6,
    )(*da_parts, tok_part, attn_gain[None, :], d_res)
    join = call(gather_kernel, sds((4, part, model), BF16), [SM] + [VM] * 4, nbytes=3e6)
    gtok_all = [gtok] + [lax.ppermute(gtok, "mp", rot(s)) for s in (1, 2, 3)]
    grad_tokens = join(at, *gtok_all).reshape(rows, model)

    out_sum = add_low(out_own, lax.ppermute(out_oth, "expert", SWAP)).reshape(4, part, model)
    out_parts = [out_sum[0]] + [lax.ppermute(out_sum[s], "mp", rot(-s)) for s in (1, 2, 3)]
    out_rows = call(output_kernel, sds((part, model), BF16), [SM] + [VM] * 5, nbytes=3e6)(
        at, *out_parts, residual
    )
    out_all = [out_rows] + [lax.ppermute(out_rows, "mp", rot(s)) for s in (1, 2, 3)]
    layer_out = join(at, *out_all).reshape(rows, model)

    mine_half = add_low(grads[0:2], lax.ppermute(grads[2:4], "dp", CORE))
    expert_grad = mine_half[0].astype(F32) + lax.ppermute(mine_half[1], "dp", YAX).astype(F32)
    grad_up = expert_grad[0]
    grad_down = expert_grad[1].transpose(0, 2, 1)

    gqkv = jnp.einsum(
        "td,ctf->cdf", relative(attn_input), dqkv, preferred_element_type=F32
    ).astype(BF16)
    grad_qkv = join_cores(reduce_all(gqkv, 1), 1).astype(F32)
    gproj = reduce_all(gproj, 1)
    gproj_parts = [gproj[0]] + [lax.ppermute(gproj[s], "mp", rot(-s)) for s in (1, 2, 3)]
    gproj_sum = functools.reduce(lambda a, b: a + b, [p.astype(F32) for p in gproj_parts])
    grad_proj = join_cores(gproj_sum.astype(BF16), 0).astype(F32)

    spot = jnp.arange(span, dtype=jnp.int32)
    far = jnp.where(spot <= seq - SUB, seq - SUB - spot, jnp.where(spot > seq, 2 * seq - spot, 0))
    bucket_of = jnp.sum((far[:, None] >= starts[None, :]).astype(jnp.int32), axis=1) - 1
    hot = (bucket_of[:, None] == jnp.arange(table, dtype=jnp.int32)[None, :]).astype(F32)
    gbias = jnp.dot(dist[:heads], hot, precision=HIGH)
    grouter = jnp.zeros((model, 128), F32)
    for s, pieces in enumerate((e_own, e_oth)):
        for b, piece in enumerate(pieces):
            grouter = grouter + lax.dot_general(
                piece, dl[s, b * part : (b + 1) * part], (((0,), (0,)), ((), ())),
                preferred_element_type=F32,
            )
    grouter = grouter[:, :experts] + grouter[:, 64 : 64 + experts]
    all_bias = lax.dynamic_update_slice(
        jnp.zeros((4 * heads, table), F32), gbias, (z * heads, 0)
    )
    small = jnp.concatenate(
        [grouter.reshape(-1), gattn[0], gmoe[0], all_bias.reshape(-1)]
    )
    size = small.shape[0]
    small = jnp.pad(small, (0, -size % 1024)).reshape(-1, 128)
    for axis, perm in (
        ("dp", CORE), ("dp", YAX), ("expert", SWAP), ("mp", SWAP + [(2, 3), (3, 2)]),
        ("mp", YAX),
    ):
        small = small + lax.ppermute(small, axis, perm)
    small = small.reshape(-1)
    cut = model * experts
    grad_router = small[:cut].reshape(model, experts)
    grad_attn = small[cut : cut + model]
    grad_moe = small[cut + model : cut + 2 * model]
    bias_sum = small[cut + 2 * model : size].reshape(4 * heads, table)
    grad_bias = lax.dynamic_slice_in_dim(bias_sum, z * heads, heads, 0).T

    return (
        layer_out, grad_tokens, grad_qkv, grad_proj, grad_bias, grad_attn, grad_moe,
        grad_router, grad_up, grad_down,
    )


def on_device(
    tokens,
    qkv_weight,
    proj_weight,
    position_bias,
    attn_gain,
    moe_gain,
    router_weight,
    expert_up,
    expert_down,
    lengths,
    routes,
    buckets,
    cotangent,
):
    row_count, model_width = tokens.shape
    local_heads = position_bias.shape[1]
    bucket_total = position_bias.shape[0]
    local_width = proj_weight.shape[0]
    head_size = local_width // local_heads
    score_scale = head_size ** (-0.5)
    seq_len = buckets.shape[0]
    owner_count = lax.axis_size("expert")
    first_row = lax.axis_index("expert") * row_count
    last_row = first_row + row_count - 1
    group_row = first_row + jnp.arange(row_count, dtype=jnp.int32)
    seq_index = group_row // seq_len
    valid = (group_row % seq_len < jnp.take(lengths, seq_index)).astype(jnp.float32)[:, None]
    bucket_ids = jnp.arange(bucket_total, dtype=jnp.int32)
    bucket_starts = jnp.sum((buckets[None, :] < bucket_ids[:, None]).astype(jnp.int32), axis=1)
    table_heads = position_bias.T

    def score_block(query_part, query_pos, key_part, key_pos):
        distance = query_pos[:, None] - key_pos[None, :]
        allowed = (distance >= 0) & (
            (query_pos // seq_len)[:, None] == (key_pos // seq_len)[None, :]
        )
        offset = jnp.clip(distance, 0, seq_len - 1)
        bucket_of = (
            jnp.sum((offset[:, :, None] >= bucket_starts[None, None, :]).astype(jnp.int32), axis=2)
            - 1
        )
        one_hot = bucket_of[:, :, None] == bucket_ids[None, None, :]
        bias_vals = jnp.sum(jnp.where(one_hot[None], table_heads[:, None, None, :], 0.0), axis=3)
        raw_scores = jnp.einsum(
            "qhd,khd->hqk", query_part, key_part, preferred_element_type=jnp.float32
        )
        scores = jnp.where(allowed[None], raw_scores * score_scale + bias_vals, NEG)
        return (scores, allowed, one_hot)

    token_values = tokens.astype(jnp.float32)
    attn_input = norm_rows(token_values, attn_gain).astype(jnp.bfloat16)
    qkv_low = jnp.einsum(
        "td,cdf->ctf", attn_input, qkv_weight, preferred_element_type=jnp.float32
    ).astype(jnp.bfloat16)
    queries = qkv_low[0].reshape(row_count, local_heads, head_size)
    key_value = jnp.concatenate([qkv_low[1], qkv_low[2]], axis=1)
    all_kv = lax.all_gather(key_value, "expert", axis=0, tiled=True)
    key_rows = all_kv.shape[0]
    key_block = math.gcd(key_rows, 1024)
    block_lo = first_row // seq_len * seq_len // key_block
    block_hi = last_row // key_block + 1

    def scores_at(step_index):
        key_start = step_index * key_block
        piece = lax.dynamic_slice_in_dim(all_kv, key_start, key_block, 0)
        keys_here = piece[:, :local_width].reshape(key_block, local_heads, head_size)
        values_here = piece[:, local_width:].reshape(key_block, local_heads, head_size)
        key_pos = key_start + jnp.arange(key_block, dtype=jnp.int32)
        scores, allowed, one_hot = score_block(queries, group_row, keys_here, key_pos)
        return (scores, allowed, one_hot, keys_here, values_here)

    def max_step(step_index, state_in):
        running_max, running_sum = state_in
        scores, allowed, one_hot, keys_here, values_here = scores_at(step_index)
        new_max = jnp.maximum(running_max, jnp.max(scores, axis=2))
        exps = jnp.where(allowed[None], jnp.exp(scores - new_max[:, :, None]), 0.0)
        return (new_max, running_sum * jnp.exp(running_max - new_max) + jnp.sum(exps, axis=2))

    start_state = (
        jnp.full((local_heads, row_count), NEG, jnp.float32),
        jnp.zeros((local_heads, row_count), jnp.float32),
    )
    running_max, running_sum = lax.fori_loop(block_lo, block_hi, max_step, start_state)
    log_total = running_max + jnp.log(running_sum)

    def value_step(step_index, mixed_sum):
        scores, allowed, one_hot, keys_here, values_here = scores_at(step_index)
        probs_low = jnp.where(allowed[None], jnp.exp(scores - log_total[:, :, None]), 0.0).astype(
            jnp.bfloat16
        )
        return mixed_sum + jnp.einsum(
            "hqk,khd->qhd", probs_low, values_here, preferred_element_type=jnp.float32
        )

    mixed_float = lax.fori_loop(
        block_lo, block_hi, value_step, jnp.zeros((row_count, local_heads, head_size), jnp.float32)
    )
    mixed_low = mixed_float.reshape(row_count, local_width).astype(jnp.bfloat16)
    attn_branch = lax.psum(
        jnp.dot(mixed_low, proj_weight, preferred_element_type=jnp.float32).astype(jnp.bfloat16),
        "mp",
    ).astype(jnp.float32)
    residual = token_values + attn_branch
    expert_input = norm_rows(residual, moe_gain).astype(jnp.bfloat16)
    logits = jnp.dot(expert_input, router_weight, preferred_element_type=jnp.float32)
    gate_weights = route_weights(logits, routes)
    expert_total = router_weight.shape[1]
    per_device = expert_up.shape[0]
    capacity = 4 * row_count // expert_total
    flat_routes = routes.reshape(-1)
    expert_ids = jnp.arange(expert_total, dtype=jnp.int32)
    expert_hits = (flat_routes[:, None] == expert_ids[None, :]).astype(jnp.int32)
    earlier_hits = jnp.cumsum(expert_hits, axis=0) - expert_hits
    slot_index = jnp.sum(earlier_hits * expert_hits, axis=1)
    target = flat_routes * capacity + slot_index
    outgoing_rows = (
        jnp.zeros((expert_total * capacity, model_width), jnp.bfloat16)
        .at[target]
        .set(jnp.repeat(expert_input, 2, axis=0))
    )
    arrived = lax.all_to_all(
        outgoing_rows.reshape(owner_count, per_device, capacity, model_width),
        "expert",
        split_axis=0,
        concat_axis=0,
        tiled=True,
    )
    pre_act = jnp.einsum("sjcd,jdf->sjcf", arrived, expert_up, preferred_element_type=jnp.float32)
    act_low = jax.nn.gelu(pre_act).astype(jnp.bfloat16)
    partial_out = jnp.einsum(
        "sjcf,jfd->sjcd", act_low, expert_down, preferred_element_type=jnp.float32
    )
    returned = lax.all_to_all(
        partial_out.astype(jnp.bfloat16), "expert", split_axis=0, concat_axis=0, tiled=True
    ).astype(partial_out.dtype)
    column_count = partial_out.shape[3]
    routed_out = returned.reshape(expert_total * capacity, column_count)[target].reshape(
        row_count, 2, column_count
    )
    moe_part = jnp.sum(gate_weights[:, :, None] * routed_out, axis=1)
    moe_branch = lax.psum(moe_part.astype(jnp.bfloat16), "mp").astype(jnp.float32)
    layer_out = (valid * (residual + moe_branch)).astype(jnp.bfloat16)
    upstream = cotangent.astype(jnp.float32) * valid
    grad_rows = (gate_weights[:, :, None] * upstream[:, None, :]).astype(jnp.bfloat16)
    back_rows = (
        jnp.zeros((expert_total * capacity, model_width), jnp.bfloat16)
        .at[target]
        .set(grad_rows.reshape(row_count * 2, model_width))
    )
    grad_arrived = lax.all_to_all(
        back_rows.reshape(owner_count, per_device, capacity, model_width),
        "expert",
        split_axis=0,
        concat_axis=0,
        tiled=True,
    )
    act_grad = jnp.einsum(
        "sjcd,jfd->sjcf", grad_arrived, expert_down, preferred_element_type=jnp.float32
    )
    gelu_pull = jax.vjp(jax.nn.gelu, pre_act)[1]
    pre_grad = gelu_pull(act_grad)[0].astype(jnp.bfloat16)
    grad_down_local = jnp.einsum(
        "sjcf,sjcd->jfd", act_low, grad_arrived, preferred_element_type=jnp.float32
    )
    grad_up_local = jnp.einsum(
        "sjcd,sjcf->jdf", arrived, pre_grad, preferred_element_type=jnp.float32
    )
    input_part = jnp.einsum(
        "sjcf,jdf->sjcd", pre_grad, expert_up, preferred_element_type=jnp.float32
    )
    input_back = lax.all_to_all(
        input_part.astype(jnp.bfloat16), "expert", split_axis=0, concat_axis=0, tiled=True
    ).astype(input_part.dtype)
    moe_input_grad = jnp.sum(
        input_back.reshape(expert_total * capacity, model_width)[target].reshape(
            row_count, 2, model_width
        ),
        axis=1,
    )
    dots_part = jnp.sum(routed_out * upstream[:, None, :], axis=2)
    moe_input_sum, router_dots = (
        lax.psum(moe_input_grad.astype(jnp.bfloat16), "mp").astype(jnp.float32),
        lax.psum(dots_part.astype(jnp.bfloat16), "mp").astype(jnp.float32),
    )
    logit_pull = jax.vjp(lambda logit_values: route_weights(logit_values, routes), logits)[1]
    logit_grad = logit_pull(router_dots)[0]
    router_float = router_weight.astype(jnp.float32)
    input_grad = moe_input_sum + jnp.dot(logit_grad, router_float.T, precision=HIGH)
    grad_router_local = jnp.dot(expert_input.astype(jnp.float32).T, logit_grad, precision=HIGH)
    norm_two_pull = jax.vjp(norm_rows, residual, moe_gain)[1]
    residual_norm_grad, grad_moe_local = norm_two_pull(input_grad)
    residual_grad = upstream + residual_norm_grad
    residual_low = residual_grad.astype(jnp.bfloat16)
    mixed_grad = jnp.einsum(
        "td,fd->tf", residual_low, proj_weight, preferred_element_type=jnp.float32
    ).astype(jnp.bfloat16)
    grad_proj_local = jnp.einsum(
        "tf,td->fd", mixed_low, residual_low, preferred_element_type=jnp.float32
    )
    mixed_grad3 = mixed_grad.reshape(row_count, local_heads, head_size)
    row_delta = jnp.sum(mixed_grad3.astype(jnp.float32) * mixed_float, axis=2).T

    def query_side(step_index, query_grad, bias_grad):
        scores, allowed, one_hot, keys_here, values_here = scores_at(step_index)
        probs = jnp.where(allowed[None], jnp.exp(scores - log_total[:, :, None]), 0.0)
        probs_grad = jnp.einsum(
            "qhd,khd->hqk", mixed_grad3, values_here, preferred_element_type=jnp.float32
        )
        score_grad = probs * (probs_grad - row_delta[:, :, None])
        bias_grad = bias_grad + jnp.sum(
            jnp.where(one_hot[None], score_grad[:, :, :, None], 0.0), axis=(1, 2)
        )
        raw_grad = (score_grad * score_scale).astype(jnp.bfloat16)
        query_grad = query_grad + jnp.einsum(
            "hqk,khd->qhd", raw_grad, keys_here, preferred_element_type=jnp.float32
        )
        return (query_grad, bias_grad, probs, raw_grad)

    query_zero = jnp.zeros((row_count, local_heads, head_size), jnp.float32)
    bias_zero = jnp.zeros((local_heads, bucket_total), jnp.float32)

    def grad_step(step_index, state_in):
        query_grad, bias_grad, probs, raw_grad = query_side(step_index, state_in[0], state_in[1])
        key_grad = jnp.einsum("hqk,qhd->khd", raw_grad, queries, preferred_element_type=jnp.float32)
        value_grad = jnp.einsum(
            "hqk,qhd->khd",
            probs.astype(jnp.bfloat16),
            mixed_grad3,
            preferred_element_type=jnp.float32,
        )
        block_terms = jnp.concatenate(
            [key_grad.reshape(key_block, local_width), value_grad.reshape(key_block, local_width)],
            axis=1,
        )
        kv_terms = lax.dynamic_update_slice_in_dim(
            state_in[2], block_terms, step_index * key_block, 0
        )
        return (query_grad, bias_grad, kv_terms)

    term_zero = jnp.zeros((key_rows, 2 * local_width), jnp.float32)
    query_grad, bias_grad, kv_terms = lax.fori_loop(
        block_lo, block_hi, grad_step, (query_zero, bias_zero, term_zero)
    )
    kv_grad = lax.psum_scatter(
        kv_terms.astype(jnp.bfloat16), "expert", scatter_dimension=0, tiled=True
    ).astype(jnp.float32)
    grad_bias_local = bias_grad.T
    qkv_grad = jnp.stack(
        [
            query_grad.reshape(row_count, local_width),
            kv_grad[:, :local_width],
            kv_grad[:, local_width:],
        ]
    ).astype(jnp.bfloat16)
    grad_qkv_local = jnp.einsum(
        "td,ctf->cdf", attn_input, qkv_grad, preferred_element_type=jnp.float32
    )
    attn_input_part = jnp.einsum(
        "ctf,cdf->td", qkv_grad, qkv_weight, preferred_element_type=jnp.float32
    )
    attn_input_grad = lax.psum(attn_input_part.astype(jnp.bfloat16), "mp").astype(jnp.float32)
    norm_one_pull = jax.vjp(norm_rows, token_values, attn_gain)[1]
    token_norm_grad, grad_attn_local = norm_one_pull(attn_input_grad)
    grad_tokens = (residual_grad + token_norm_grad).astype(jnp.bfloat16)
    shared_grads = lax.psum(
        (
            grad_qkv_local,
            grad_proj_local,
            grad_bias_local,
            grad_attn_local,
            grad_moe_local,
            grad_router_local,
        ),
        ("dp", "expert"),
    )
    grad_up, grad_down = (
        lax.psum_scatter(
            grad_up_local.astype(jnp.bfloat16), "dp", scatter_dimension=1, tiled=True
        ).astype(jnp.float32),
        lax.psum_scatter(
            grad_down_local.astype(jnp.bfloat16), "dp", scatter_dimension=2, tiled=True
        ).astype(jnp.float32),
    )
    return (
        layer_out,
        grad_tokens,
        shared_grads[0],
        shared_grads[1],
        shared_grads[2],
        shared_grads[3],
        shared_grads[4],
        shared_grads[5],
        grad_up,
        grad_down,
    )


def choose(*args):
    tokens, position_bias, buckets = args[0], args[3], args[11]
    rows = tokens.shape[0]
    head_size = args[2].shape[0] // position_bias.shape[1]
    fits = (
        lax.axis_size("expert") == 2
        and lax.axis_size("mp") == 4
        and lax.axis_size("dp") == 4
        and buckets.shape[0] == 2 * rows
        and rows % 768 == 0
        and args[9].shape[0] == 1
        and head_size == 64
        and args[6].shape[1] <= 64
    )
    return fast_device(*args) if fits else on_device(*args)


def solution(mesh):
    placed = (
        P(("dp", "expert"), None),
        P(None, None, "mp"),
        P("mp", None),
        P(None, "mp"),
        P(),
        P(),
        P(),
        P("expert", None, "mp"),
        P("expert", "mp", None),
        P("dp"),
        P(("dp", "expert"), None),
        P(),
        P(("dp", "expert"), None),
    )
    return jax.shard_map(
        choose,
        mesh=mesh,
        in_specs=placed,
        out_specs=(
            P(("dp", "expert"), None),
            P(("dp", "expert"), None),
            P(None, None, "mp"),
            P("mp", None),
            P(None, "mp"),
            P(),
            P(),
            P(),
            P("expert", "dp", "mp"),
            P("expert", "mp", "dp"),
        ),
        check_vma=False,
    )
```
